32 devices in a mesh: view: 16 (over z, y, x), head: 2 (over core).
Axes of the slice: x: 2, y: 2, z: 4, core: 2. Of those that a mesh axis runs over, the one named last changes fastest.
Arguments:
- query_tokens: bfloat16 [4096, 1024], P('view'), may hold values from -360 to 360
- image_tokens: bfloat16 [16384, 1024], P('view'), may hold values from -6 to 6
- w_query: bfloat16 [1024, 1024], P(None, 'head'), may hold values from -0.1875 to 0.1875
- w_key: bfloat16 [1024, 1024], P(None, 'head'), may hold values from -0.1875 to 0.1875
- w_value: bfloat16 [1024, 1024], P(None, 'head'), may hold values from -0.1875 to 0.1875
- w_out: bfloat16 [1024, 1024], P('head'), may hold values from -0.1875 to 0.1875
- vis_list: int32 [32, 12], P('view'), may hold values from 0 to 127, as said below
- vis_count: int32 [32], P('view'), may hold values from 8 to 12
Outputs:
- attended: bfloat16 [4096, 1024], P('view', 'head')
The draws below stay inside these ranges and needn't reach their ends.
Inputs may be any that keep to these rules, and one draw needn't show every extreme that they name: `vis_list`: entry j of row b names a global image block (block g holds image tokens g * 128 onward); the first vis_count[b] entries are the visible ones, the rest padding. All entries of one row lie on different devices of view. Among all entries of the 2 rows held by one device, those lying on one source device name the same block.
All inputs are finite; a program needn't handle non-finite values.
Results may differ from the reference program's by a relative error of at most 0.0085.
The reference program's roundings to bfloat16 on the way (of `queries`, `probs` and `context`) count: a program that leaves them out, or rounds other values in their place, can miss the bound.
Values may be sent and summed in bfloat16 or wider, within the bound.
A program may use at most 64 MiB of HBM per device.

```python
import math
import jax
import jax.numpy as jnp
from jax import lax

D = 1024
HEADS = 8
HEAD_DIM = 128
BLOCK = 128
QB_DEV = 2
BLK_DEV = 8
MAXVIS = 12
TRI = 4096
IMG = 16384
QBLK = 32


def visibility(key):
    base = jax.random.fold_in(key, 11)
    pick_key, order_key, count_key, full_key = jax.random.split(base, 4)
    device_count = QBLK // QB_DEV
    chosen_block = jax.random.randint(pick_key, (device_count, device_count), 0, BLK_DEV)
    ranking = jax.random.randint(order_key, (QBLK, device_count), 0, 1 << 16) * device_count + jnp.arange(device_count)[None, :]
    sources = jnp.argsort(ranking, axis=1)[:, :MAXVIS].astype(jnp.int32)
    owner = jnp.arange(QBLK) // QB_DEV
    blocks = jnp.take_along_axis(chosen_block[owner], sources, axis=1)
    block_ids = (sources * BLK_DEV + blocks).astype(jnp.int32)
    counts = jax.random.randint(count_key, (QBLK,), device_count // 2, MAXVIS + 1)
    fullest = jax.random.randint(full_key, (), 0, QBLK)
    counts = jnp.where(jnp.arange(QBLK) == fullest, MAXVIS, counts).astype(jnp.int32)
    return (block_ids, counts)


def draw_vis_list(key, part):
    return visibility(key)[0]


def draw_vis_count(key, part):
    return visibility(key)[1]


def draw_query_tokens(key, part):
    base_key = jax.random.fold_in(jax.random.fold_in(key, 3), 0)
    values = jax.random.truncated_normal(base_key, -6.0, 6.0, (TRI, D), jnp.float32)
    return values.astype(jnp.bfloat16)


def steps_of(own_key, dims, cuts, smallest, top_value):
    def one(position, shards_of):
        heights = jax.random.uniform(jax.random.fold_in(jax.random.fold_in(own_key, 6), position), (shards_of,), jnp.float32, smallest / len(cuts), top_value / len(cuts))
        return jnp.repeat(jnp.exp(heights), dims[position] // shards_of).reshape((-1,) + (1,) * (len(dims) - position - 1))

    loudness = one(*cuts[0])
    for cut in cuts[1:]:
        loudness = loudness * one(*cut)
    return loudness


def normal_values(own_key, shape, deviation, limit, shards=(), held_as=jnp.bfloat16):
    values = jax.random.normal(own_key, shape, jnp.float32) * deviation
    if len(shards) > 0:
        values = steps_of(own_key, shape, shards, -0.22, 0.18) * values
    return jnp.clip(values, min=-limit, max=limit).astype(held_as)


def setup_inputs(seed: int = 0) -> dict:
    streams_of = jax.random.split(jax.random.key(seed), 9)
    return {
        "query_tokens": draw_query_tokens(jax.random.fold_in(streams_of[8], 71), 0),
        "image_tokens": normal_values(streams_of[1], (IMG, D), 1.0, 6.0, ((0, 16),)),
        "w_query": normal_values(streams_of[2], (D, D), D ** -0.5, 0.1875, ((1, 2),)),
        "w_key": normal_values(streams_of[3], (D, D), D ** -0.5, 0.1875, ((1, 2),)),
        "w_value": normal_values(streams_of[4], (D, D), D ** -0.5, 0.1875, ((1, 2),)),
        "w_out": normal_values(streams_of[5], (D, D), D ** -0.5, 0.1875, ((0, 2),)),
        "vis_list": draw_vis_list(jax.random.fold_in(streams_of[8], 71), 0),
        "vis_count": draw_vis_count(jax.random.fold_in(streams_of[8], 71), 0),
    }


def reference(query_tokens, image_tokens, w_query, w_key, w_value, w_out, vis_list, vis_count):
    queries = jnp.dot(query_tokens, w_query, preferred_element_type=jnp.float32).astype(jnp.bfloat16)
    image_keys = jnp.dot(image_tokens, w_key, preferred_element_type=jnp.float32).astype(jnp.bfloat16)
    image_values = jnp.dot(image_tokens, w_value, preferred_element_type=jnp.float32).astype(jnp.bfloat16)
    key_blocks = image_keys.reshape(-1, BLOCK, D)
    value_blocks = image_values.reshape(-1, BLOCK, D)
    query_heads = queries.reshape(-1, BLOCK, HEADS, HEAD_DIM)
    positions = jnp.arange(MAXVIS * BLOCK, dtype=jnp.int32) // BLOCK

    def attend_block(inputs):
        query_rows, block_ids, visible_count = inputs
        block_keys = jnp.take(key_blocks, block_ids.astype(jnp.int32), axis=0).reshape(MAXVIS * BLOCK, HEADS, HEAD_DIM).astype(jnp.float32)
        block_values = jnp.take(value_blocks, block_ids.astype(jnp.int32), axis=0).reshape(MAXVIS * BLOCK, HEADS, HEAD_DIM).astype(jnp.float32)
        scores = jnp.einsum('ihd,khd->hik', query_rows.astype(jnp.float32), block_keys) * (1.0 / math.sqrt(HEAD_DIM))
        allowed = (positions < visible_count)[None, None, :]
        peak = lax.optimization_barrier(jnp.max(jnp.where(allowed, scores, -1e+30), axis=2, keepdims=True))
        raised = jnp.where(allowed, jnp.exp(scores - peak), 0.0)
        probs = (raised / lax.optimization_barrier(jnp.sum(raised, axis=2, keepdims=True))).astype(jnp.bfloat16)
        probs = lax.optimization_barrier(probs)
        context = jnp.einsum('hik,khd->ihd', probs.astype(jnp.float32), block_values)
        return context.astype(jnp.bfloat16).reshape(BLOCK, D)
    context = lax.map(attend_block, (query_heads, vis_list, vis_count)).reshape(-1, D)
    return jnp.dot(context, w_out, preferred_element_type=jnp.float32).astype(jnp.bfloat16)
```

```python
import functools
import math

import jax
import jax.numpy as jnp
from jax import lax
from jax.experimental import pallas as pl
from jax.experimental.pallas import tpu as pltpu
from jax.sharding import PartitionSpec as P

HEAD_DIM = 128
BLOCK = 128
GROUP = 4
MESH = pl.DeviceIdType.MESH
HIDDEN = -1e30


def offset_of(slot, view_count):
    return (view_count - slot) % view_count


def partner(index, offset, view_count):
    result, bit = 0, 1
    while bit < view_count:
        flip = (index // bit + offset // bit) % 2
        result = result + flip * bit
        bit *= 2
    return result


def kernel(
    n,
    heads,
    qt_hbm,
    x_hbm,
    wq_hbm,
    wk_hbm,
    wv_hbm,
    wo_hbm,
    own_ref,
    ask_ref,
    bias_ref,
    out_ref,
    x_vm,
    qt_vm,
    wq_vm,
    wk_vm,
    wv_vm,
    wo_all,
    asked_vm,
    asked_sm,
    picked,
    arrived,
    q_vm,
    k_vm,
    v_vm,
    peak_vm,
    total_vm,
    acc_vm,
    ctx_all,
    load_sem,
    ask_send,
    ask_recv,
    asked_sem,
    tok_send,
    tok_recv,
    fwd_send,
    fwd_recv,
    wo_send,
    wo_recv,
    ctx_send,
    ctx_recv,
):
    me = lax.axis_index("view")
    core = lax.axis_index("head")
    rows, width = out_ref.shape
    panel = wq_vm.shape[1]
    head_count = panel // HEAD_DIM
    depth = x_vm.shape[-1]
    groups = n // GROUP
    query_blocks = rows // BLOCK
    scale = 1.0 / math.sqrt(HEAD_DIM)

    def peer(slot):
        return (partner(me, offset_of(slot, n), n), core)

    def sibling(step):
        return (core + step) % heads

    def before(step):
        return (core + heads - step) % heads

    barrier = pltpu.get_barrier_semaphore()
    for slot in range(1, n):
        pl.semaphore_signal(barrier, inc=1, device_id=peer(slot), device_id_type=MESH)
    for step in range(1, heads):
        pl.semaphore_signal(
            barrier, inc=1, device_id=(me, sibling(step)), device_id_type=MESH
        )

    loads = [
        pltpu.make_async_copy(source, target, load_sem.at[position])
        for position, (source, target) in enumerate(
            [
                (x_hbm, x_vm),
                (qt_hbm, qt_vm),
                (wq_hbm, wq_vm),
                (wk_hbm, wk_vm),
                (wv_hbm, wv_vm),
                (
                    wo_hbm.at[:, pl.ds(pl.multiple_of(core * width, 128), width)],
                    wo_all.at[core],
                ),
            ]
        )
    ]
    for load in loads:
        load.start()
    pl.semaphore_wait(barrier, n - 1 + heads - 1)

    def ask(slot):
        return pltpu.make_async_remote_copy(
            src_ref=ask_ref.at[slot],
            dst_ref=asked_vm.at[slot],
            send_sem=ask_send.at[slot],
            recv_sem=ask_recv.at[slot],
            device_id=peer(slot),
            device_id_type=MESH,
        )

    def token(slot):
        return pltpu.make_async_remote_copy(
            src_ref=picked.at[slot],
            dst_ref=arrived.at[slot, core],
            send_sem=tok_send.at[slot],
            recv_sem=tok_recv.at[slot],
            device_id=peer(slot),
            device_id_type=MESH,
        )

    def forward(slot, step, part):
        return pltpu.make_async_remote_copy(
            src_ref=arrived.at[slot, part],
            dst_ref=arrived.at[slot, part],
            send_sem=fwd_send.at[slot, step],
            recv_sem=fwd_recv.at[slot, step],
            device_id=(me, sibling(step)),
            device_id_type=MESH,
        )

    def weight(step, part, columns):
        return pltpu.make_async_remote_copy(
            src_ref=wo_hbm.at[:, pl.ds(pl.multiple_of(columns * width, 128), width)],
            dst_ref=wo_all.at[part],
            send_sem=wo_send.at[step],
            recv_sem=wo_recv.at[step],
            device_id=(me, sibling(step)),
            device_id_type=MESH,
        )

    def context(step, head, part):
        lanes = pl.ds(head * HEAD_DIM, HEAD_DIM)
        return pltpu.make_async_remote_copy(
            src_ref=ctx_all.at[part, :, lanes],
            dst_ref=ctx_all.at[part, :, lanes],
            send_sem=ctx_send.at[step, head],
            recv_sem=ctx_recv.at[step, head],
            device_id=(me, sibling(step)),
            device_id_type=MESH,
        )

    for slot in range(1, n):
        ask(slot).start()
    for slot in range(1, n):
        ask(slot).wait_recv()
    rest = pl.ds(1, n - 1)
    fetch = pltpu.make_async_copy(asked_vm.at[rest], asked_sm.at[rest], asked_sem)
    fetch.start()
    loads[0].wait()
    fetch.wait()
    for slot in range(1, n):
        picked[slot] = x_vm[asked_sm[slot, 0, 0], core]
    for slot in range(1, n):
        token(slot).start()
    for step in range(1, heads):
        weight(step, core, sibling(step)).start()
    arrived[0] = x_vm[own_ref[0]]

    loads[1].wait()
    loads[2].wait()
    q_vm[...] = jnp.dot(
        qt_vm[...], wq_vm[...], preferred_element_type=jnp.float32
    ).astype(q_vm.dtype)
    peak_vm[...] = jnp.full_like(peak_vm, -3e38)
    total_vm[...] = jnp.zeros_like(total_vm)
    acc_vm[...] = jnp.zeros_like(acc_vm)
    loads[3].wait()
    loads[4].wait()

    def take_in(group):
        for member in range(GROUP):
            slot = group * GROUP + member

            @pl.when(slot > 0)
            def _():
                token(slot).wait_recv()
                for step in range(1, heads):
                    forward(slot, step, core).start()

    def settle(group):
        for member in range(GROUP):
            slot = group * GROUP + member

            @pl.when(slot > 0)
            def _():
                for step in range(1, heads):
                    forward(slot, step, before(step)).wait_recv()

    def attend(group):
        tokens = arrived[pl.ds(group * GROUP, GROUP)].reshape(GROUP * BLOCK, depth)
        k_vm[...] = jnp.dot(
            tokens, wk_vm[...], preferred_element_type=jnp.float32
        ).astype(k_vm.dtype)
        v_vm[...] = jnp.dot(
            tokens, wv_vm[...], preferred_element_type=jnp.float32
        ).astype(v_vm.dtype)
        bias = bias_ref[group]
        for head in range(head_count):
            lanes = pl.ds(head * HEAD_DIM, HEAD_DIM)
            scores = lax.dot_general(
                q_vm[:, lanes],
                k_vm[:, lanes],
                (((1,), (1,)), ((), ())),
                preferred_element_type=jnp.float32,
            )
            scores = scores * scale
            scores = (
                scores.reshape(query_blocks, BLOCK, GROUP * BLOCK) + bias
            ).reshape(rows, GROUP * BLOCK)
            old = peak_vm[head]
            new = jnp.maximum(old, jnp.max(scores, axis=1, keepdims=True))
            fade = jnp.exp(old - new)
            raised = jnp.exp(scores - new[:, :1])
            folded = raised[:, :BLOCK]
            for member in range(1, GROUP):
                folded = folded + raised[:, member * BLOCK : (member + 1) * BLOCK]
            peak_vm[head] = new
            total_vm[head] = total_vm[head] * fade + folded
            acc_vm[head] = acc_vm[head] * fade + jnp.dot(
                raised.astype(v_vm.dtype),
                v_vm[:, lanes],
                preferred_element_type=jnp.float32,
            )

    take_in(0)

    def advance(group, carry):
        @pl.when(group + 1 < groups)
        def _():
            take_in(group + 1)

        settle(group)
        attend(group)
        return carry

    lax.fori_loop(0, groups, advance, 0)

    for head in range(head_count):
        lanes = pl.ds(head * HEAD_DIM, HEAD_DIM)
        row_sum = jnp.sum(total_vm[head], axis=1, keepdims=True)
        ctx_all[core, :, lanes] = (acc_vm[head] / row_sum).astype(ctx_all.dtype)
        for step in range(1, heads):
            context(step, head, core).start()
    loads[5].wait()
    result = jnp.dot(
        ctx_all[core], wo_all[core], preferred_element_type=jnp.float32
    )
    for step in range(1, heads):
        part = before(step)
        weight(step, part, core).wait_recv()
        for head in range(head_count):
            context(step, head, part).wait_recv()
        result = result + jnp.dot(
            ctx_all[part], wo_all[part], preferred_element_type=jnp.float32
        )
    out_ref[...] = result.astype(out_ref.dtype)

    for slot in range(1, n):
        ask(slot).wait_send()
        token(slot).wait_send()
        for step in range(1, heads):
            forward(slot, step, core).wait_send()
    for step in range(1, heads):
        weight(step, core, sibling(step)).wait_send()
        for head in range(head_count):
            context(step, head, core).wait_send()


def per_device(query_tokens, image_tokens, w_query, w_key, w_value, w_out, vis_list, vis_count):
    n = lax.axis_size("view")
    heads = lax.axis_size("head")
    me = lax.axis_index("view")
    rows, depth = query_tokens.shape
    panel = w_query.shape[1]
    head_count = panel // HEAD_DIM
    width = w_out.shape[1] // heads
    block_count = image_tokens.shape[0] // BLOCK
    part_rows = BLOCK // heads
    query_blocks = vis_list.shape[0]
    groups = n // GROUP

    slots = jnp.arange(n, dtype=jnp.int32)
    sources = partner(me, offset_of(slots, n), n)
    matches = (vis_list // block_count)[:, :, None] == sources[None, None, :]
    listed = jnp.arange(vis_list.shape[1], dtype=jnp.int32)[None, :] < vis_count[:, None]
    sourced = jnp.any(matches & listed[:, :, None], axis=1)
    wanted = jnp.max(
        jnp.where(matches, (vis_list % block_count)[:, :, None], 0), axis=(0, 1)
    ).astype(jnp.int32)
    ask = jnp.broadcast_to(wanted[:, None, None], (n, 1, 128))
    bias = jnp.where(sourced, 0.0, HIDDEN).astype(jnp.float32)
    bias = jnp.repeat(bias, BLOCK, axis=1).reshape(query_blocks, groups, 1, GROUP * BLOCK)
    bias = jnp.transpose(bias, (1, 0, 2, 3))

    anywhere = pl.BlockSpec(memory_space=pl.ANY)
    vmem = pl.BlockSpec(memory_space=pltpu.VMEM)
    dtype = image_tokens.dtype
    dma = pltpu.SemaphoreType.DMA
    return pl.pallas_call(
        functools.partial(kernel, n, heads),
        out_shape=jax.ShapeDtypeStruct((rows, width), dtype),
        in_specs=[anywhere] * 6 + [pl.BlockSpec(memory_space=pltpu.SMEM), vmem, vmem],
        out_specs=vmem,
        scratch_shapes=[
            pltpu.VMEM((block_count, heads, part_rows, depth), dtype),
            pltpu.VMEM((rows, depth), dtype),
            pltpu.VMEM((depth, panel), dtype),
            pltpu.VMEM((depth, panel), dtype),
            pltpu.VMEM((depth, panel), dtype),
            pltpu.VMEM((heads, panel, width), dtype),
            pltpu.VMEM((n, 1, 128), jnp.int32),
            pltpu.SMEM((n, 1, 128), jnp.int32),
            pltpu.VMEM((n, part_rows, depth), dtype),
            pltpu.VMEM((n, heads, part_rows, depth), dtype),
            pltpu.VMEM((rows, panel), dtype),
            pltpu.VMEM((GROUP * BLOCK, panel), dtype),
            pltpu.VMEM((GROUP * BLOCK, panel), dtype),
            pltpu.VMEM((head_count, rows, HEAD_DIM), jnp.float32),
            pltpu.VMEM((head_count, rows, HEAD_DIM), jnp.float32),
            pltpu.VMEM((head_count, rows, HEAD_DIM), jnp.float32),
            pltpu.VMEM((heads, rows, panel), dtype),
            dma((6,)),
            dma((n,)),
            dma((n,)),
            dma,
            dma((n,)),
            dma((n,)),
            dma((n, heads)),
            dma((n, heads)),
            dma((heads,)),
            dma((heads,)),
            dma((heads, head_count)),
            dma((heads, head_count)),
        ],
        compiler_params=pltpu.CompilerParams(
            collective_id=0, has_side_effects=True, vmem_limit_bytes=52 * 2**20
        ),
    )(
        query_tokens,
        image_tokens.reshape(block_count, heads, part_rows, depth),
        w_query,
        w_key,
        w_value,
        w_out,
        wanted[:1],
        ask,
        bias,
    )


def solution(mesh):
    return jax.shard_map(
        per_device,
        mesh=mesh,
        in_specs=(
            P("view", None),
            P("view", None),
            P(None, "head"),
            P(None, "head"),
            P(None, "head"),
            P("head", None),
            P("view", None),
            P("view"),
        ),
        out_specs=P("view", "head"),
        check_vma=False,
    )
```

```python
import functools
import math

import jax
import jax.numpy as jnp
from jax import lax
from jax.experimental import pallas as pl
from jax.experimental.pallas import tpu as pltpu
from jax.sharding import PartitionSpec as P

HEAD_DIM = 128
BLOCK = 128
GROUP = 4
MESH = pl.DeviceIdType.MESH
HIDDEN = -1e30


def offset_of(slot, view_count):
    half = view_count // 2
    return slot % half + half * (1 - slot // half)


def flipped(index, offset, view_count):
    result, bit = 0, 1
    while bit < view_count:
        flip = (index // bit + offset // bit) % 2
        result = result + flip * bit
        bit *= 2
    return result


def kernel(
    n,
    heads,
    qt_hbm,
    x_hbm,
    wq_hbm,
    wk_hbm,
    wv_hbm,
    wo_hbm,
    own_ref,
    ask_ref,
    bias_ref,
    out_ref,
    x_vm,
    qt_vm,
    wq_vm,
    wk_vm,
    wv_vm,
    wo_all,
    asked_vm,
    asked_sm,
    picked,
    arrived,
    q_vm,
    k_vm,
    v_vm,
    peak_vm,
    total_vm,
    acc_vm,
    ctx_all,
    bias_in,
    part_out,
    part_in,
    stat_out,
    stat_in,
    load_sem,
    ask_send,
    ask_recv,
    asked_sem,
    tok_send,
    tok_recv,
    fwd_send,
    fwd_recv,
    wo_send,
    wo_recv,
    ctx_send,
    ctx_recv,
    mate_send,
    mate_recv,
):
    me = lax.axis_index("view")
    core = lax.axis_index("head")
    rows, width = out_ref.shape
    panel = wq_vm.shape[1]
    head_count = panel // HEAD_DIM
    depth = x_vm.shape[-1]
    half = n // 2
    set_groups = half // GROUP
    query_blocks = rows // BLOCK
    scale = 1.0 / math.sqrt(HEAD_DIM)

    def peer(slot):
        return (flipped(me, offset_of(slot, n), n), core)

    def holder(slot):
        return (flipped(me, slot % half, n), core)

    mate = (flipped(me, half, n), core)

    def sibling(step):
        return (core + step) % heads

    def before(step):
        return (core + heads - step) % heads

    barrier = pltpu.get_barrier_semaphore()
    asked_slots = [slot for slot in range(n) if slot != half]
    sent_slots = [slot for slot in range(n) if slot % half]
    for slot in asked_slots:
        pl.semaphore_signal(barrier, inc=1, device_id=peer(slot), device_id_type=MESH)
    for step in range(1, heads):
        pl.semaphore_signal(
            barrier, inc=1, device_id=(me, sibling(step)), device_id_type=MESH
        )

    loads = [
        pltpu.make_async_copy(source, target, load_sem.at[position])
        for position, (source, target) in enumerate(
            [
                (x_hbm, x_vm),
                (qt_hbm, qt_vm),
                (wq_hbm, wq_vm),
                (wk_hbm, wk_vm),
                (wv_hbm, wv_vm),
                (
                    wo_hbm.at[:, pl.ds(pl.multiple_of(core * width, 128), width)],
                    wo_all.at[core],
                ),
            ]
        )
    ]
    for load in loads:
        load.start()
    pl.semaphore_wait(barrier, len(asked_slots) + heads - 1)

    def ask(slot):
        return pltpu.make_async_remote_copy(
            src_ref=ask_ref.at[slot],
            dst_ref=asked_vm.at[slot],
            send_sem=ask_send.at[slot],
            recv_sem=ask_recv.at[slot],
            device_id=peer(slot),
            device_id_type=MESH,
        )

    def token(slot):
        return pltpu.make_async_remote_copy(
            src_ref=picked.at[slot],
            dst_ref=arrived.at[slot, core],
            send_sem=tok_send.at[slot],
            recv_sem=tok_recv.at[slot],
            device_id=holder(slot),
            device_id_type=MESH,
        )

    def forward(slot, step, part):
        return pltpu.make_async_remote_copy(
            src_ref=arrived.at[slot, part],
            dst_ref=arrived.at[slot, part],
            send_sem=fwd_send.at[slot, step],
            recv_sem=fwd_recv.at[slot, step],
            device_id=(me, sibling(step)),
            device_id_type=MESH,
        )

    def weight(step, part, columns):
        return pltpu.make_async_remote_copy(
            src_ref=wo_hbm.at[:, pl.ds(pl.multiple_of(columns * width, 128), width)],
            dst_ref=wo_all.at[part],
            send_sem=wo_send.at[step],
            recv_sem=wo_recv.at[step],
            device_id=(me, sibling(step)),
            device_id_type=MESH,
        )

    def context(step, head, part):
        lanes = pl.ds(head * HEAD_DIM, HEAD_DIM)
        return pltpu.make_async_remote_copy(
            src_ref=ctx_all.at[part, :, lanes],
            dst_ref=ctx_all.at[part, :, lanes],
            send_sem=ctx_send.at[step, head],
            recv_sem=ctx_recv.at[step, head],
            device_id=(me, sibling(step)),
            device_id_type=MESH,
        )

    def to_mate(position, source, target):
        return pltpu.make_async_remote_copy(
            src_ref=source,
            dst_ref=target,
            send_sem=mate_send.at[position],
            recv_sem=mate_recv.at[position],
            device_id=mate,
            device_id_type=MESH,
        )

    def partial(head):
        lanes = pl.ds(head * HEAD_DIM, HEAD_DIM)
        return to_mate(3 + head, part_out.at[:, lanes], part_in.at[:, lanes])

    lend = to_mate(0, q_vm.at[1], q_vm.at[0])
    hint = to_mate(1, bias_ref.at[pl.ds(0, set_groups)], bias_in)
    stats = to_mate(2, stat_out, stat_in)

    for slot in asked_slots:
        ask(slot).start()
    hint.start()
    loads[1].wait()
    loads[2].wait()
    q_vm[1] = jnp.dot(
        qt_vm[...], wq_vm[...], preferred_element_type=jnp.float32
    ).astype(q_vm.dtype)
    lend.start()
    loads[0].wait()
    for slot in asked_slots:
        ask(slot).wait_recv()
    fetches = [
        pltpu.make_async_copy(
            asked_vm.at[pl.ds(start, size)],
            asked_sm.at[pl.ds(start, size)],
            asked_sem.at[position],
        )
        for position, (start, size) in enumerate([(0, half), (half + 1, half - 1)])
    ]
    for fetch in fetches:
        fetch.start()
    for fetch in fetches:
        fetch.wait()
    for slot in sent_slots:
        picked[slot] = x_vm[asked_sm[slot, 0, 0], core]
    for slot in sent_slots:
        token(slot).start()
    for step in range(1, heads):
        weight(step, core, sibling(step)).start()
    arrived[0] = x_vm[asked_sm[0, 0, 0]]
    arrived[half] = x_vm[own_ref[0]]
    loads[3].wait()
    loads[4].wait()

    def take_in(group):
        for member in range(GROUP):
            slot = group * GROUP + member

            @pl.when(slot % half > 0)
            def _():
                token(slot).wait_recv()
                for step in range(1, heads):
                    forward(slot, step, core).start()

    def settle(group):
        for member in range(GROUP):
            slot = group * GROUP + member

            @pl.when(slot % half > 0)
            def _():
                for step in range(1, heads):
                    forward(slot, step, before(step)).wait_recv()

    def attend(group, own, bias):
        tokens = arrived[pl.ds(group * GROUP, GROUP)].reshape(GROUP * BLOCK, depth)
        k_vm[...] = jnp.dot(
            tokens, wk_vm[...], preferred_element_type=jnp.float32
        ).astype(k_vm.dtype)
        v_vm[...] = jnp.dot(
            tokens, wv_vm[...], preferred_element_type=jnp.float32
        ).astype(v_vm.dtype)
        for head in range(head_count):
            lanes = pl.ds(head * HEAD_DIM, HEAD_DIM)
            scores = lax.dot_general(
                q_vm[own, :, lanes],
                k_vm[:, lanes],
                (((1,), (1,)), ((), ())),
                preferred_element_type=jnp.float32,
            )
            scores = scores * scale
            scores = (
                scores.reshape(query_blocks, BLOCK, GROUP * BLOCK) + bias
            ).reshape(rows, GROUP * BLOCK)
            old = peak_vm[head]
            new = jnp.maximum(old, jnp.max(scores, axis=1, keepdims=True))
            fade = jnp.exp(old - new)
            raised = jnp.exp(scores - new[:, :1])
            folded = raised[:, :BLOCK]
            for member in range(1, GROUP):
                folded = folded + raised[:, member * BLOCK : (member + 1) * BLOCK]
            peak_vm[head] = new
            total_vm[head] = total_vm[head] * fade + folded
            acc_vm[head] = acc_vm[head] * fade + jnp.dot(
                raised.astype(v_vm.dtype),
                v_vm[:, lanes],
                preferred_element_type=jnp.float32,
            )

    def reset():
        peak_vm[...] = jnp.full_like(peak_vm, -3e38)
        total_vm[...] = jnp.zeros_like(total_vm)
        acc_vm[...] = jnp.zeros_like(acc_vm)

    def row_sums(head):
        folded = jnp.sum(total_vm[head], axis=1, keepdims=True)
        return jnp.broadcast_to(folded, (rows, HEAD_DIM))

    def attend_set(own):
        first = own * set_groups
        last = first + set_groups
        reset()
        take_in(first)

        def advance(group, carry):
            @pl.when(group + 1 < last)
            def _():
                take_in(group + 1)

            settle(group)
            attend(group, own, bias_ref[group] if own else bias_in[group])
            return carry

        lax.fori_loop(first, last, advance, 0)

    lend.wait_recv()
    hint.wait_recv()
    attend_set(0)
    for head in range(head_count):
        lanes = pl.ds(head * HEAD_DIM, HEAD_DIM)
        part_out[:, lanes] = acc_vm[head].astype(part_out.dtype)
        partial(head).start()
        stat_out[pl.ds(2 * head, 1), :] = peak_vm[head].T[:1]
        stat_out[pl.ds(2 * head + 1, 1), :] = row_sums(head).T[:1]
    stats.start()
    attend_set(1)
    stats.wait_recv()
    for head in range(head_count):
        lanes = pl.ds(head * HEAD_DIM, HEAD_DIM)
        partial(head).wait_recv()

        def spread(row):
            return jnp.broadcast_to(stat_in[pl.ds(row, 1), :], (HEAD_DIM, rows)).T

        peak, mate_peak = peak_vm[head], spread(2 * head)
        top = jnp.maximum(peak, mate_peak)
        weight_own = jnp.exp(peak - top)
        weight_mate = jnp.exp(mate_peak - top)
        row_sum = row_sums(head) * weight_own + spread(2 * head + 1) * weight_mate
        merged = acc_vm[head] * weight_own + part_in[:, lanes] * weight_mate
        ctx_all[core, :, lanes] = (merged / row_sum).astype(ctx_all.dtype)
        for step in range(1, heads):
            context(step, head, core).start()
    loads[5].wait()
    result = jnp.dot(
        ctx_all[core], wo_all[core], preferred_element_type=jnp.float32
    )
    for step in range(1, heads):
        part = before(step)
        weight(step, part, core).wait_recv()
        for head in range(head_count):
            context(step, head, part).wait_recv()
        result = result + jnp.dot(
            ctx_all[part], wo_all[part], preferred_element_type=jnp.float32
        )
    out_ref[...] = result.astype(out_ref.dtype)

    for slot in asked_slots:
        ask(slot).wait_send()
    for slot in sent_slots:
        token(slot).wait_send()
        for step in range(1, heads):
            forward(slot, step, core).wait_send()
    for copy in [lend, hint, stats] + [partial(head) for head in range(head_count)]:
        copy.wait_send()
    for step in range(1, heads):
        weight(step, core, sibling(step)).wait_send()
        for head in range(head_count):
            context(step, head, core).wait_send()


def per_device(query_tokens, image_tokens, w_query, w_key, w_value, w_out, vis_list, vis_count):
    n = lax.axis_size("view")
    heads = lax.axis_size("head")
    me = lax.axis_index("view")
    rows, depth = query_tokens.shape
    panel = w_query.shape[1]
    head_count = panel // HEAD_DIM
    width = w_out.shape[1] // heads
    block_count = image_tokens.shape[0] // BLOCK
    part_rows = BLOCK // heads
    query_blocks = vis_list.shape[0]
    groups = n // GROUP

    slots = jnp.arange(n, dtype=jnp.int32)
    sources = flipped(me, offset_of(slots, n), n)
    matches = (vis_list // block_count)[:, :, None] == sources[None, None, :]
    listed = jnp.arange(vis_list.shape[1], dtype=jnp.int32)[None, :] < vis_count[:, None]
    sourced = jnp.any(matches & listed[:, :, None], axis=1)
    wanted = jnp.max(
        jnp.where(matches, (vis_list % block_count)[:, :, None], 0), axis=(0, 1)
    ).astype(jnp.int32)
    ask = jnp.broadcast_to(wanted[:, None, None], (n, 1, 128))
    bias = jnp.where(sourced, 0.0, HIDDEN).astype(jnp.float32)
    bias = jnp.repeat(bias, BLOCK, axis=1).reshape(query_blocks, groups, 1, GROUP * BLOCK)
    bias = jnp.transpose(bias, (1, 0, 2, 3))

    anywhere = pl.BlockSpec(memory_space=pl.ANY)
    vmem = pl.BlockSpec(memory_space=pltpu.VMEM)
    dtype = image_tokens.dtype
    dma = pltpu.SemaphoreType.DMA
    return pl.pallas_call(
        functools.partial(kernel, n, heads),
        out_shape=jax.ShapeDtypeStruct((rows, width), dtype),
        in_specs=[anywhere] * 6 + [pl.BlockSpec(memory_space=pltpu.SMEM), vmem, vmem],
        out_specs=vmem,
        scratch_shapes=[
            pltpu.VMEM((block_count, heads, part_rows, depth), dtype),
            pltpu.VMEM((rows, depth), dtype),
            pltpu.VMEM((depth, panel), dtype),
            pltpu.VMEM((depth, panel), dtype),
            pltpu.VMEM((depth, panel), dtype),
            pltpu.VMEM((heads, panel, width), dtype),
            pltpu.VMEM((n, 1, 128), jnp.int32),
            pltpu.SMEM((n, 1, 128), jnp.int32),
            pltpu.VMEM((n, part_rows, depth), dtype),
            pltpu.VMEM((n, heads, part_rows, depth), dtype),
            pltpu.VMEM((2, rows, panel), dtype),
            pltpu.VMEM((GROUP * BLOCK, panel), dtype),
            pltpu.VMEM((GROUP * BLOCK, panel), dtype),
            pltpu.VMEM((head_count, rows, HEAD_DIM), jnp.float32),
            pltpu.VMEM((head_count, rows, HEAD_DIM), jnp.float32),
            pltpu.VMEM((head_count, rows, HEAD_DIM), jnp.float32),
            pltpu.VMEM((heads, rows, panel), dtype),
            pltpu.VMEM((groups // 2,) + bias.shape[1:], jnp.float32),
            pltpu.VMEM((rows, panel), dtype),
            pltpu.VMEM((rows, panel), dtype),
            pltpu.VMEM((2 * head_count, rows), jnp.float32),
            pltpu.VMEM((2 * head_count, rows), jnp.float32),
            dma((6,)),
            dma((n,)),
            dma((n,)),
            dma((2,)),
            dma((n,)),
            dma((n,)),
            dma((n, heads)),
            dma((n, heads)),
            dma((heads,)),
            dma((heads,)),
            dma((heads, head_count)),
            dma((heads, head_count)),
            dma((3 + head_count,)),
            dma((3 + head_count,)),
        ],
        compiler_params=pltpu.CompilerParams(
            collective_id=0, has_side_effects=True, vmem_limit_bytes=60 * 2**20
        ),
    )(
        query_tokens,
        image_tokens.reshape(block_count, heads, part_rows, depth),
        w_query,
        w_key,
        w_value,
        w_out,
        wanted[n // 2 : n // 2 + 1],
        ask,
        bias,
    )


def solution(mesh):
    return jax.shard_map(
        per_device,
        mesh=mesh,
        in_specs=(
            P("view", None),
            P("view", None),
            P(None, "head"),
            P(None, "head"),
            P(None, "head"),
            P("head", None),
            P("view", None),
            P("view"),
        ),
        out_specs=P("view", "head"),
        check_vma=False,
    )
```

```python
import functools
import math

import jax
import jax.numpy as jnp
from jax import lax
from jax.experimental import pallas as pl
from jax.experimental.pallas import tpu as pltpu
from jax.sharding import PartitionSpec as P

HEAD_DIM = 128
BLOCK = 128
GROUP = 2
MESH = pl.DeviceIdType.MESH
HIDDEN = -1e30


def offset_of(slot, view_count):
    half = view_count // 2
    return slot % half + half * (1 - slot // half)


def flipped(index, offset, view_count):
    result, bit = 0, 1
    while bit < view_count:
        flip = (index // bit + offset // bit) % 2
        result = result + flip * bit
        bit *= 2
    return result


def kernel(
    n,
    heads,
    qt_hbm,
    x_hbm,
    wq_hbm,
    wk_hbm,
    wv_hbm,
    wo_hbm,
    own_ref,
    ask_ref,
    bias_ref,
    out_ref,
    x_vm,
    qt_vm,
    wq_vm,
    wk_vm,
    wv_vm,
    wo_all,
    asked_vm,
    asked_sm,
    picked,
    arrived,
    q_vm,
    k_vm,
    v_vm,
    peak_vm,
    total_vm,
    acc_vm,
    ctx_all,
    bias_in,
    part_out,
    part_in,
    stat_out,
    stat_in,
    load_sem,
    ask_send,
    ask_recv,
    asked_sem,
    tok_send,
    tok_recv,
    fwd_send,
    fwd_recv,
    wo_send,
    wo_recv,
    ctx_send,
    ctx_recv,
    mate_send,
    mate_recv,
):
    me = lax.axis_index("view")
    core = lax.axis_index("head")
    rows, width = out_ref.shape
    panel = wq_vm.shape[1]
    head_count = panel // HEAD_DIM
    depth = x_vm.shape[-1]
    half = n // 2
    set_groups = half // GROUP
    query_blocks = rows // BLOCK
    scale = 1.0 / math.sqrt(HEAD_DIM)

    def peer(slot):
        return (flipped(me, offset_of(slot, n), n), core)

    def holder(slot):
        return (flipped(me, slot % half, n), core)

    mate = (flipped(me, half, n), core)

    def sibling(step):
        return (core + step) % heads

    def before(step):
        return (core + heads - step) % heads

    barrier = pltpu.get_barrier_semaphore()
    asked_slots = [slot for slot in range(n) if slot != half]
    sent_slots = [slot for slot in range(n) if slot % half]
    for slot in asked_slots:
        pl.semaphore_signal(barrier, inc=1, device_id=peer(slot), device_id_type=MESH)
    for step in range(1, heads):
        pl.semaphore_signal(
            barrier, inc=1, device_id=(me, sibling(step)), device_id_type=MESH
        )

    loads = [
        pltpu.make_async_copy(source, target, load_sem.at[position])
        for position, (source, target) in enumerate(
            [
                (x_hbm, x_vm),
                (qt_hbm, qt_vm),
                (wq_hbm, wq_vm),
                (wk_hbm, wk_vm),
                (wv_hbm, wv_vm),
                (
                    wo_hbm.at[:, pl.ds(pl.multiple_of(core * width, 128), width)],
                    wo_all.at[core],
                ),
            ]
        )
    ]
    for position in (1, 2, 0, 3, 4, 5):
        loads[position].start()
    loads[1].wait()
    loads[2].wait()
    q_vm[1] = jnp.dot(
        qt_vm[...], wq_vm[...], preferred_element_type=jnp.float32
    ).astype(q_vm.dtype)
    pl.semaphore_wait(barrier, len(asked_slots) + heads - 1)

    def ask(slot):
        return pltpu.make_async_remote_copy(
            src_ref=ask_ref.at[slot],
            dst_ref=asked_vm.at[slot],
            send_sem=ask_send.at[slot],
            recv_sem=ask_recv.at[slot],
            device_id=peer(slot),
            device_id_type=MESH,
        )

    def token(slot):
        return pltpu.make_async_remote_copy(
            src_ref=picked.at[slot],
            dst_ref=arrived.at[slot, core],
            send_sem=tok_send.at[slot],
            recv_sem=tok_recv.at[slot],
            device_id=holder(slot),
            device_id_type=MESH,
        )

    def forward(slot, step, part):
        return pltpu.make_async_remote_copy(
            src_ref=arrived.at[slot, part],
            dst_ref=arrived.at[slot, part],
            send_sem=fwd_send.at[slot, step],
            recv_sem=fwd_recv.at[slot, step],
            device_id=(me, sibling(step)),
            device_id_type=MESH,
        )

    def weight(step, part, columns):
        return pltpu.make_async_remote_copy(
            src_ref=wo_hbm.at[:, pl.ds(pl.multiple_of(columns * width, 128), width)],
            dst_ref=wo_all.at[part],
            send_sem=wo_send.at[step],
            recv_sem=wo_recv.at[step],
            device_id=(me, sibling(step)),
            device_id_type=MESH,
        )

    def context(step, head, part):
        lanes = pl.ds(head * HEAD_DIM, HEAD_DIM)
        return pltpu.make_async_remote_copy(
            src_ref=ctx_all.at[part, :, lanes],
            dst_ref=ctx_all.at[part, :, lanes],
            send_sem=ctx_send.at[step, head],
            recv_sem=ctx_recv.at[step, head],
            device_id=(me, sibling(step)),
            device_id_type=MESH,
        )

    def to_mate(position, source, target):
        return pltpu.make_async_remote_copy(
            src_ref=source,
            dst_ref=target,
            send_sem=mate_send.at[position],
            recv_sem=mate_recv.at[position],
            device_id=mate,
            device_id_type=MESH,
        )

    def partial(head):
        lanes = pl.ds(head * HEAD_DIM, HEAD_DIM)
        return to_mate(3 + head, part_out.at[:, lanes], part_in.at[:, lanes])

    lend = to_mate(0, q_vm.at[1], q_vm.at[0])
    hint = to_mate(1, bias_ref.at[pl.ds(0, set_groups)], bias_in)
    stats = to_mate(2, stat_out, stat_in)

    for slot in asked_slots:
        ask(slot).start()
    lend.start()
    hint.start()
    loads[0].wait()
    for slot in asked_slots:
        ask(slot).wait_recv()
    fetches = [
        pltpu.make_async_copy(
            asked_vm.at[pl.ds(start, size)],
            asked_sm.at[pl.ds(start, size)],
            asked_sem.at[position],
        )
        for position, (start, size) in enumerate([(0, half), (half + 1, half - 1)])
    ]
    for fetch in fetches:
        fetch.start()
    for fetch in fetches:
        fetch.wait()
    for slot in sent_slots:
        picked[slot] = x_vm[asked_sm[slot, 0, 0], core]
    for slot in sent_slots:
        token(slot).start()
    for step in range(1, heads):
        weight(step, core, sibling(step)).start()
    arrived[0] = x_vm[asked_sm[0, 0, 0]]
    arrived[half] = x_vm[own_ref[0]]
    loads[3].wait()
    loads[4].wait()

    def take_in(group):
        for member in range(GROUP):
            slot = group * GROUP + member

            @pl.when(slot % half > 0)
            def _():
                token(slot).wait_recv()
                for step in range(1, heads):
                    forward(slot, step, core).start()

    def settle(group):
        for member in range(GROUP):
            slot = group * GROUP + member

            @pl.when(slot % half > 0)
            def _():
                for step in range(1, heads):
                    forward(slot, step, before(step)).wait_recv()

    def attend(group, own, bias):
        tokens = arrived[pl.ds(group * GROUP, GROUP)].reshape(GROUP * BLOCK, depth)
        k_vm[...] = jnp.dot(
            tokens, wk_vm[...], preferred_element_type=jnp.float32
        ).astype(k_vm.dtype)
        v_vm[...] = jnp.dot(
            tokens, wv_vm[...], preferred_element_type=jnp.float32
        ).astype(v_vm.dtype)
        for head in range(head_count):
            lanes = pl.ds(head * HEAD_DIM, HEAD_DIM)
            scores = lax.dot_general(
                q_vm[own, :, lanes],
                k_vm[:, lanes],
                (((1,), (1,)), ((), ())),
                preferred_element_type=jnp.float32,
            )
            scores = scores * scale
            scores = (
                scores.reshape(query_blocks, BLOCK, GROUP * BLOCK) + bias
            ).reshape(rows, GROUP * BLOCK)
            old = peak_vm[head]
            new = jnp.maximum(old, jnp.max(scores, axis=1, keepdims=True))
            fade = jnp.exp(old - new)
            raised = jnp.exp(scores - new[:, :1])
            folded = raised[:, :BLOCK]
            for member in range(1, GROUP):
                folded = folded + raised[:, member * BLOCK : (member + 1) * BLOCK]
            peak_vm[head] = new
            total_vm[head] = total_vm[head] * fade + folded
            acc_vm[head] = acc_vm[head] * fade + jnp.dot(
                raised.astype(v_vm.dtype),
                v_vm[:, lanes],
                preferred_element_type=jnp.float32,
            )

    def reset():
        peak_vm[...] = jnp.full_like(peak_vm, -3e38)
        total_vm[...] = jnp.zeros_like(total_vm)
        acc_vm[...] = jnp.zeros_like(acc_vm)

    def row_sums(head):
        folded = jnp.sum(total_vm[head], axis=1, keepdims=True)
        return jnp.broadcast_to(folded, (rows, HEAD_DIM))

    def attend_set(own):
        first = own * set_groups
        last = first + set_groups
        reset()
        take_in(first)

        def advance(group, carry):
            @pl.when(group + 1 < last)
            def _():
                take_in(group + 1)

            settle(group)
            attend(group, own, bias_ref[group] if own else bias_in[group])
            return carry

        lax.fori_loop(first, last, advance, 0)

    lend.wait_recv()
    hint.wait_recv()
    attend_set(0)
    for head in range(head_count):
        lanes = pl.ds(head * HEAD_DIM, HEAD_DIM)
        part_out[:, lanes] = acc_vm[head].astype(part_out.dtype)
        partial(head).start()
        stat_out[pl.ds(2 * head, 1), :] = peak_vm[head].T[:1]
        stat_out[pl.ds(2 * head + 1, 1), :] = row_sums(head).T[:1]
    stats.start()
    attend_set(1)
    stats.wait_recv()
    for head in range(head_count):
        lanes = pl.ds(head * HEAD_DIM, HEAD_DIM)
        partial(head).wait_recv()

        def spread(row):
            return jnp.broadcast_to(stat_in[pl.ds(row, 1), :], (HEAD_DIM, rows)).T

        peak, mate_peak = peak_vm[head], spread(2 * head)
        top = jnp.maximum(peak, mate_peak)
        weight_own = jnp.exp(peak - top)
        weight_mate = jnp.exp(mate_peak - top)
        row_sum = row_sums(head) * weight_own + spread(2 * head + 1) * weight_mate
        merged = acc_vm[head] * weight_own + part_in[:, lanes] * weight_mate
        ctx_all[core, :, lanes] = (merged / row_sum).astype(ctx_all.dtype)
        for step in range(1, heads):
            context(step, head, core).start()
    loads[5].wait()
    result = jnp.dot(
        ctx_all[core], wo_all[core], preferred_element_type=jnp.float32
    )
    for step in range(1, heads):
        part = before(step)
        weight(step, part, core).wait_recv()
        for head in range(head_count):
            context(step, head, part).wait_recv()
        result = result + jnp.dot(
            ctx_all[part], wo_all[part], preferred_element_type=jnp.float32
        )
    out_ref[...] = result.astype(out_ref.dtype)

    for slot in asked_slots:
        ask(slot).wait_send()
    for slot in sent_slots:
        token(slot).wait_send()
        for step in range(1, heads):
            forward(slot, step, core).wait_send()
    for copy in [lend, hint, stats] + [partial(head) for head in range(head_count)]:
        copy.wait_send()
    for step in range(1, heads):
        weight(step, core, sibling(step)).wait_send()
        for head in range(head_count):
            context(step, head, core).wait_send()


def per_device(query_tokens, image_tokens, w_query, w_key, w_value, w_out, vis_list, vis_count):
    n = lax.axis_size("view")
    heads = lax.axis_size("head")
    me = lax.axis_index("view")
    rows, depth = query_tokens.shape
    panel = w_query.shape[1]
    head_count = panel // HEAD_DIM
    width = w_out.shape[1] // heads
    block_count = image_tokens.shape[0] // BLOCK
    part_rows = BLOCK // heads
    query_blocks = vis_list.shape[0]
    groups = n // GROUP

    slots = jnp.arange(n, dtype=jnp.int32)
    sources = flipped(me, offset_of(slots, n), n)
    matches = (vis_list // block_count)[:, :, None] == sources[None, None, :]
    listed = jnp.arange(vis_list.shape[1], dtype=jnp.int32)[None, :] < vis_count[:, None]
    sourced = jnp.any(matches & listed[:, :, None], axis=1)
    wanted = jnp.max(
        jnp.where(matches, (vis_list % block_count)[:, :, None], 0), axis=(0, 1)
    ).astype(jnp.int32)
    ask = jnp.broadcast_to(wanted[:, None, None], (n, 1, 128))
    bias = jnp.where(sourced, 0.0, HIDDEN).astype(jnp.float32)
    bias = jnp.repeat(bias, BLOCK, axis=1).reshape(query_blocks, groups, 1, GROUP * BLOCK)
    bias = jnp.transpose(bias, (1, 0, 2, 3))

    anywhere = pl.BlockSpec(memory_space=pltpu.HBM)
    vmem = pl.BlockSpec(memory_space=pltpu.VMEM)
    dtype = image_tokens.dtype
    dma = pltpu.SemaphoreType.DMA
    return pl.pallas_call(
        functools.partial(kernel, n, heads),
        out_shape=jax.ShapeDtypeStruct((rows, width), dtype),
        in_specs=[anywhere] * 6 + [pl.BlockSpec(memory_space=pltpu.SMEM), vmem, vmem],
        out_specs=vmem,
        scratch_shapes=[
            pltpu.VMEM((block_count, heads, part_rows, depth), dtype),
            pltpu.VMEM((rows, depth), dtype),
            pltpu.VMEM((depth, panel), dtype),
            pltpu.VMEM((depth, panel), dtype),
            pltpu.VMEM((depth, panel), dtype),
            pltpu.VMEM((heads, panel, width), dtype),
            pltpu.VMEM((n, 1, 128), jnp.int32),
            pltpu.SMEM((n, 1, 128), jnp.int32),
            pltpu.VMEM((n, part_rows, depth), dtype),
            pltpu.VMEM((n, heads, part_rows, depth), dtype),
            pltpu.VMEM((2, rows, panel), dtype),
            pltpu.VMEM((GROUP * BLOCK, panel), dtype),
            pltpu.VMEM((GROUP * BLOCK, panel), dtype),
            pltpu.VMEM((head_count, rows, HEAD_DIM), jnp.float32),
            pltpu.VMEM((head_count, rows, HEAD_DIM), jnp.float32),
            pltpu.VMEM((head_count, rows, HEAD_DIM), jnp.float32),
            pltpu.VMEM((heads, rows, panel), dtype),
            pltpu.VMEM((groups // 2,) + bias.shape[1:], jnp.float32),
            pltpu.VMEM((rows, panel), dtype),
            pltpu.VMEM((rows, panel), dtype),
            pltpu.VMEM((2 * head_count, rows), jnp.float32),
            pltpu.VMEM((2 * head_count, rows), jnp.float32),
            dma((6,)),
            dma((n,)),
            dma((n,)),
            dma((2,)),
            dma((n,)),
            dma((n,)),
            dma((n, heads)),
            dma((n, heads)),
            dma((heads,)),
            dma((heads,)),
            dma((heads, head_count)),
            dma((heads, head_count)),
            dma((3 + head_count,)),
            dma((3 + head_count,)),
        ],
        compiler_params=pltpu.CompilerParams(
            collective_id=0, has_side_effects=True, vmem_limit_bytes=int(53.6 * 2**20)
        ),
    )(
        query_tokens,
        image_tokens.reshape(block_count, heads, part_rows, depth),
        w_query,
        w_key,
        w_value,
        w_out,
        wanted[n // 2 : n // 2 + 1],
        ask,
        bias,
    )


def solution(mesh):
    return jax.shard_map(
        per_device,
        mesh=mesh,
        in_specs=(
            P("view", None),
            P("view", None),
            P(None, "head"),
            P(None, "head"),
            P(None, "head"),
            P("head", None),
            P("view", None),
            P("view"),
        ),
        out_specs=P("view", "head"),
        check_vma=False,
    )
```
